32 devices in a mesh: tok: 8 (over z, x), col: 4 (over y, core).
Axes of the slice: x: 2, y: 2, z: 4, core: 2. Of those that a mesh axis runs over, the one named last changes fastest.
Arguments:
- tokens: bfloat16 [2560, 4096], P('tok', 'col'), may hold values from -16 to 16
- w_query: bfloat16 [4096, 2048], P(None, 'col'), may hold values from -0.09375 to 0.09375
- w_key: bfloat16 [4096, 512], P(None, 'col'), may hold values from -0.09375 to 0.09375
- w_value: bfloat16 [4096, 512], P(None, 'col'), may hold values from -0.09375 to 0.09375
- w_out: bfloat16 [2048, 4096], P('col'), may hold values from -0.125 to 0.125
- block_ids: int32 [16, 40, 16], P('col', 'tok'), may hold values from 0 to 39, as said below
- block_counts: int32 [16, 40], P('col', 'tok'), may hold values from 1 to 16, as said below
Outputs:
- mixed: bfloat16 [2560, 4096], P('tok', 'col')
The draws below stay inside these ranges and needn't reach their ends.
Inputs may be any that keep to these rules, and one draw needn't show every extreme that they name: block_ids[h, b, 0] = b; the slots below block_counts[h, b] hold distinct blocks none after b; later slots hold block numbers that are not read. block_counts[h, b] <= b + 1; densities differ from head to head, and some row of some head uses all 16 slots.
All inputs are finite; a program needn't handle non-finite values.
Results may differ from the reference program's by a relative error of at most 0.012.
Values may be sent and summed in bfloat16 or wider, within the bound.
No kernel may reach another device: no remote copies, remote signals or barrier semaphores. Data moves between devices by JAX's collectives and lax.ppermute only.
A program may use at most 64 MiB of HBM per device.

```python
import jax
import jax.numpy as jnp
from jax import lax

D = 4096
HQ = 16
HK = 4
HEAD_SIZE = 128
BLK = 64
NSEL = 16
TOKENS = 2560
NBLK = 40
GROUP = 4


def draw_tokens(key, part):
    first_key = jax.random.fold_in(key, 0)
    result = jnp.clip(jax.random.normal(first_key, (TOKENS, D), jnp.float32), -6.0, 6.0)
    return result.astype(jnp.bfloat16)


def pattern(key):
    base = jax.random.fold_in(key, 7)
    order_key, count_key, head_key, hot_key = jax.random.split(base, 4)
    blocks = jnp.arange(NBLK, dtype=jnp.int32)
    logit_scores = jax.random.randint(order_key, (HQ, NBLK, NBLK), 0, 2 ** 20, dtype=jnp.int32) * NBLK + blocks[None, None, :]
    later = blocks[None, None, :] > blocks[None, :, None]
    logit_scores = jnp.where(later, 2 ** 30, logit_scores)
    logit_scores = jnp.where(blocks[None, None, :] == blocks[None, :, None], -1, logit_scores)
    chosen = jnp.argsort(logit_scores, axis=-1, stable=True)[..., :NSEL].astype(jnp.int32)
    most = jax.random.randint(head_key, (HQ,), max(NSEL // 4, 1), NSEL + 1, dtype=jnp.int32)
    hot = jax.random.randint(hot_key, (), 0, HQ, dtype=jnp.int32)
    most = jnp.where(jnp.arange(HQ, dtype=jnp.int32) == hot, NSEL, most)
    counts = jax.random.randint(count_key, (HQ, NBLK), 1, NSEL + 1, dtype=jnp.int32)
    counts = jnp.minimum(counts, most[:, None])
    counts = jnp.where(blocks[None, :] == NBLK - 1, most[:, None], counts)
    counts = jnp.minimum(counts, blocks[None, :] + 1)
    return (chosen, counts.astype(jnp.int32))


def draw_block_ids(key, part):
    return pattern(key)[0]


def draw_block_counts(key, part):
    return pattern(key)[1]


def block_levels(key, dims, shards, least, high):
    gain, own = 1.0, jax.random.fold_in(key, 6)
    for axis_at, parts in shards:
        heights = jnp.exp(jax.random.uniform(jax.random.fold_in(own, axis_at), (parts,), jnp.float32, least / len(shards), high / len(shards)))
        gain = gain * jnp.repeat(heights, dims[axis_at] // parts).reshape([-1 if axis == axis_at else 1 for axis in range(len(dims))])
    return gain


def centred(rng, dims, spread, limit, cuts=(), kind=jnp.bfloat16):
    loudness = block_levels(rng, dims, cuts, -0.22, 0.18) if cuts else 1.0
    values = jax.random.normal(rng, dims, jnp.float32) * spread * loudness
    return jnp.minimum(jnp.maximum(values, -limit), limit).astype(kind)


def setup_inputs(seed: int = 0) -> dict:
    streams_of = jax.random.split(jax.random.key(seed), 8)
    return {
        "tokens": draw_tokens(jax.random.fold_in(streams_of[7], 71), 0),
        "w_query": centred(streams_of[1], (D, HQ * HEAD_SIZE), D ** -0.5, 0.09375, ((1, 4),)),
        "w_key": centred(streams_of[2], (D, HK * HEAD_SIZE), D ** -0.5, 0.09375, ((1, 4),)),
        "w_value": centred(streams_of[3], (D, HK * HEAD_SIZE), D ** -0.5, 0.09375, ((1, 4),)),
        "w_out": centred(streams_of[4], (HQ * HEAD_SIZE, D), (HQ * HEAD_SIZE) ** -0.5, 0.125, ((0, 4),)),
        "block_ids": draw_block_ids(jax.random.fold_in(streams_of[7], 71), 0),
        "block_counts": draw_block_counts(jax.random.fold_in(streams_of[7], 71), 0),
    }


rope_base = 500000.0


def rotate(field, positions):
    half = field.shape[-1] // 2
    freq = rope_base ** (-jnp.arange(half, dtype=jnp.float32) / half)
    angle = positions[:, None] * freq[None, :]
    cosine = jnp.cos(angle)[:, None, :]
    sine = jnp.sin(angle)[:, None, :]
    first = field[..., :half]
    second = field[..., half:]
    return jnp.concatenate([first * cosine - second * sine, second * cosine + first * sine], axis=-1)


def attend_blocks(query_rows, keys, values, chosen, counts, qblock):
    number = query_rows.shape[0]
    selected_keys = keys[chosen].reshape(number, NSEL * BLK, HEAD_SIZE)
    selected_values = values[chosen].reshape(number, NSEL * BLK, HEAD_SIZE)
    logit_scores = jnp.einsum('rzs,ris->rzi', query_rows.astype(jnp.float32), selected_keys.astype(jnp.float32)) * (HEAD_SIZE ** -0.5)
    live = jnp.arange(NSEL, dtype=jnp.int32)[None, :] < counts[:, None]
    diagonal = chosen == qblock[:, None]
    inner = jnp.arange(BLK, dtype=jnp.int32)
    causal = inner[None, :] <= inner[:, None]
    allowed = live[:, None, :, None] & (jnp.logical_not(diagonal)[:, None, :, None] | causal[None, :, None, :])
    allowed = allowed.reshape(number, BLK, NSEL * BLK)
    masked = jnp.where(allowed, logit_scores, -1e30)
    highest = jnp.max(masked, axis=-1, keepdims=True)
    weights = jnp.where(allowed, jnp.exp(masked - highest), 0.0)
    total = jnp.sum(weights, axis=-1)
    rounded_scores = weights.astype(jnp.bfloat16)
    summed_weights = jnp.einsum('unh,uhm->unm', rounded_scores.astype(jnp.float32), selected_values.astype(jnp.float32))
    return (summed_weights / total[..., None]).astype(jnp.bfloat16)


def reference(tokens, w_query, w_key, w_value, w_out, block_ids, block_counts):
    positions = jnp.arange(TOKENS, dtype=jnp.float32)
    query_raw = jnp.dot(tokens, w_query, preferred_element_type=jnp.float32).reshape(TOKENS, HQ, HEAD_SIZE)
    key_raw = jnp.dot(tokens, w_key, preferred_element_type=jnp.float32).reshape(TOKENS, HK, HEAD_SIZE)
    query_rows = rotate(query_raw, positions).astype(jnp.bfloat16)
    keys = rotate(key_raw, positions).astype(jnp.bfloat16)
    values = jnp.dot(tokens, w_value, preferred_element_type=jnp.float32).astype(jnp.bfloat16).reshape(TOKENS, HK, HEAD_SIZE)
    qblock = jnp.arange(NBLK, dtype=jnp.int32)

    def one_head(head):
        kv_head = head // GROUP
        head_queries = lax.dynamic_index_in_dim(query_rows, head, 1, keepdims=False).reshape(NBLK, BLK, HEAD_SIZE)
        head_keys = lax.dynamic_index_in_dim(keys, kv_head, 1, keepdims=False).reshape(NBLK, BLK, HEAD_SIZE)
        head_values = lax.dynamic_index_in_dim(values, kv_head, 1, keepdims=False).reshape(NBLK, BLK, HEAD_SIZE)
        result = attend_blocks(head_queries, head_keys, head_values, block_ids[head], block_counts[head], qblock)
        return result.reshape(TOKENS, HEAD_SIZE)

    heads = lax.map(one_head, jnp.arange(HQ, dtype=jnp.int32))
    attended = jnp.transpose(heads, (1, 0, 2)).reshape(TOKENS, HQ * HEAD_SIZE)
    return jnp.dot(attended, w_out, preferred_element_type=jnp.float32).astype(jnp.bfloat16)
```

```python
import functools

import jax
import jax.numpy as jnp
from jax import lax
from jax.experimental import pallas as pl
from jax.experimental.pallas import tpu as pltpu
from jax.sharding import PartitionSpec as P

HEAD_SIZE = 128
BLK = 64
GROUP_BLOCKS = 4
ROPE_BASE = 500000.0
NEG = -1e30


def angles(positions):
    half = HEAD_SIZE // 2
    freq = ROPE_BASE ** (-jnp.arange(half, dtype=jnp.float32) / half)
    angle = positions[:, None] * freq[None, :]
    return jnp.cos(angle), jnp.sin(angle)


def rotate(field, cosine, sine):
    half = field.shape[-1] // 2
    first = field[..., :half]
    second = field[..., half:]
    cosine = cosine[:, None, :]
    sine = sine[:, None, :]
    return jnp.concatenate(
        [first * cosine - second * sine, second * cosine + first * sine], axis=-1
    )


def attend_kernel(heads, qblocks, nsel, part_rows, *refs):
    offsets_ref, counts_ref, q_ref = refs[:3]
    parts = refs[3 : 3 + len(part_rows)]
    out_ref, kv_ref, sem = refs[3 + len(part_rows) :]
    at = 0
    copies = []
    for index, (part, rows) in enumerate(zip(parts, part_rows)):
        copy = pltpu.make_async_copy(part, kv_ref.at[pl.ds(at, rows)], sem.at[index])
        copy.start()
        copies.append(copy)
        at += rows
    for copy in copies:
        copy.wait()
    width = GROUP_BLOCKS * BLK
    groups = nsel // GROUP_BLOCKS
    scale = HEAD_SIZE**-0.5

    def one_qblock(qb, carry):
        lane = lax.broadcasted_iota(jnp.int32, (BLK, width), 1)
        row = lax.broadcasted_iota(jnp.int32, (BLK, width), 0)
        rows = pl.ds(pl.multiple_of(qb * BLK, BLK), BLK)
        for head in range(heads):
            columns = slice(head * HEAD_SIZE, (head + 1) * HEAD_SIZE)
            query = q_ref[rows, columns]
            place = head * qblocks + qb
            count = counts_ref[place]
            scores = []
            values = []
            for group in range(groups):
                pieces = []
                for slot in range(GROUP_BLOCKS):
                    start = offsets_ref[place * nsel + group * GROUP_BLOCKS + slot]
                    pieces.append(kv_ref[pl.ds(pl.multiple_of(start, BLK), BLK), :])
                both = jnp.concatenate(pieces, axis=0)
                values.append(both[:, HEAD_SIZE:])
                score = lax.dot_general(
                    query,
                    both[:, :HEAD_SIZE],
                    (((1,), (1,)), ((), ())),
                    preferred_element_type=jnp.float32,
                )
                allowed = lane < (count - group * GROUP_BLOCKS) * BLK
                if group == 0:
                    allowed = allowed & ((lane >= BLK) | (lane <= row))
                scores.append(jnp.where(allowed, score, NEG))
            highest = jnp.max(
                functools.reduce(jnp.maximum, scores), axis=-1, keepdims=True
            )
            total = jnp.zeros((BLK, width), jnp.float32)
            summed = jnp.zeros((BLK, HEAD_SIZE), jnp.float32)
            for score, value in zip(scores, values):
                weights = jnp.exp((score - highest) * scale)
                total = total + weights
                summed = summed + jnp.dot(
                    weights.astype(jnp.bfloat16),
                    value,
                    preferred_element_type=jnp.float32,
                )
            total = jnp.sum(total, axis=-1, keepdims=True)
            out_ref[rows, columns] = (summed / total).astype(jnp.bfloat16)
        return carry

    lax.fori_loop(0, qblocks, one_qblock, 0)


def attend(offsets, counts, query, parts, heads, qblocks, nsel):
    part_rows = tuple(part.shape[0] for part in parts)
    return pl.pallas_call(
        functools.partial(attend_kernel, heads, qblocks, nsel, part_rows),
        out_shape=jax.ShapeDtypeStruct(query.shape, jnp.bfloat16),
        in_specs=[pl.BlockSpec(memory_space=pltpu.SMEM)] * 2
        + [pl.BlockSpec(memory_space=pltpu.VMEM)]
        + [pl.BlockSpec(memory_space=pl.ANY)] * len(parts),
        out_specs=pl.BlockSpec(memory_space=pltpu.VMEM),
        scratch_shapes=[
            pltpu.VMEM((sum(part_rows), 2 * HEAD_SIZE), jnp.bfloat16),
            pltpu.SemaphoreType.DMA((len(parts),)),
        ],
        compiler_params=pltpu.CompilerParams(vmem_limit_bytes=24 << 20),
        cost_estimate=pl.CostEstimate(
            flops=4 * heads * qblocks * nsel * BLK * BLK * HEAD_SIZE,
            transcendentals=heads * qblocks * nsel * BLK * BLK,
            bytes_accessed=sum(part_rows) * 4 * HEAD_SIZE,
        ),
    )(offsets, counts, query, *parts)


def on_device(mesh, tokens, w_query, w_key, w_value, w_out, block_ids, block_counts):
    cols, toks = mesh.shape["col"], mesh.shape["tok"]
    tok_rows, feat = tokens.shape
    heads = w_query.shape[1] // HEAD_SIZE
    qblocks, nsel = block_ids.shape[1:]
    col = lax.axis_index("col")
    tok = lax.axis_index("tok")
    lines = toks // 2

    def over_col(value, flip):
        return lax.ppermute(value, "col", [(i, i ^ flip) for i in range(cols)])

    def across(value):
        return lax.ppermute(value, "tok", [(i, i ^ 1) for i in range(toks)])

    def up(value, steps):
        return lax.ppermute(
            value, "tok", [(i, i + 2 * steps) for i in range(toks - 2 * steps)]
        )

    first = (qblocks + 1) // 2 * BLK
    spans = [(0, first), (first, tok_rows)]
    far_parts = [over_col(tokens[a:b], 2) for a, b in spans]
    near = over_col(tokens, 1)
    send_near = lax.dynamic_slice_in_dim(w_out, (col ^ 1) * feat, feat, 1)
    send_far = lax.dynamic_slice_in_dim(w_out, (col ^ 3) * feat, feat, 1)
    partner_out = over_col(jnp.concatenate([send_near, send_far], 1), 1)
    own_out_near = lax.dynamic_slice_in_dim(w_out, col * feat, feat, 1)
    own_out_far = lax.dynamic_slice_in_dim(w_out, (col ^ 2) * feat, feat, 1)

    weights = jnp.concatenate([w_query, w_key, w_value], axis=1)

    def rows_of(flip):
        return lax.dynamic_slice_in_dim(weights, (col ^ flip) * feat, feat, 0)

    def dot(a, b):
        return jnp.dot(a, b, preferred_element_type=jnp.float32)

    near_sum = dot(tokens, rows_of(0)) + dot(near, rows_of(1))
    far_first, far_second = rows_of(2), rows_of(3)

    positions = (tok * tok_rows + jnp.arange(tok_rows, dtype=jnp.int32)).astype(
        jnp.float32
    )
    cosine, sine = angles(positions)
    live = (
        jnp.arange(nsel, dtype=jnp.int32)[None, None, :] < block_counts[:, :, None]
    )
    chosen = jnp.where(live, block_ids, block_ids[:, :, :1])
    owner, inside = chosen // qblocks, chosen % qblocks
    slot = (tok // 2 - owner // 2) * 2 + ((owner % 2) ^ (tok % 2))
    offsets = (slot * tok_rows + inside * BLK).reshape(-1)
    counts = block_counts.reshape(-1)

    query_parts = []
    shards = [[] for _ in range(toks)]
    for (a, b), far in zip(spans, far_parts):
        rows = b - a
        opposite = over_col(far, 1)
        product = near_sum[a:b] + dot(far, far_first) + dot(opposite, far_second)
        turned = rotate(
            product[:, : (heads + 1) * HEAD_SIZE].reshape(rows, heads + 1, HEAD_SIZE),
            cosine[a:b],
            sine[a:b],
        ).astype(jnp.bfloat16)
        query_parts.append(turned[:, :heads].reshape(rows, heads * HEAD_SIZE))
        value = product[:, (heads + 1) * HEAD_SIZE :].astype(jnp.bfloat16)
        pair = jnp.concatenate([turned[:, heads], value], axis=1)
        for line in range(lines):
            moved = up(pair, line) if line else pair
            shards[2 * line].append(moved)
            shards[2 * line + 1].append(across(moved))
    query = jnp.concatenate(query_parts, axis=0)
    parts = [piece for shard in shards for piece in shard]
    attended = attend(offsets, counts, query, parts, heads, qblocks, nsel)
    partner = over_col(attended, 1)
    inner = w_out.shape[0]
    outs = []
    for a, b in spans:
        sent = dot(attended[a:b], own_out_far) + dot(partner[a:b], partner_out[:, feat:])
        arrived = over_col(sent.astype(jnp.bfloat16), 2)
        kept = dot(attended[a:b], own_out_near) + dot(partner[a:b], partner_out[:, :feat])
        outs.append((kept + arrived.astype(jnp.float32)).astype(jnp.bfloat16))
    return jnp.concatenate(outs, axis=0)


def solution(mesh):
    in_specs = (
        P("tok", "col"),
        P(None, "col"),
        P(None, "col"),
        P(None, "col"),
        P("col", None),
        P("col", "tok", None),
        P("col", "tok"),
    )
    return jax.shard_map(
        functools.partial(on_device, mesh),
        mesh=mesh,
        in_specs=in_specs,
        out_specs=P("tok", "col"),
        check_vma=False,
    )
```

```python
import functools

import jax
import jax.numpy as jnp
from jax import lax
from jax.experimental import pallas as pl
from jax.experimental.pallas import tpu as pltpu
from jax.sharding import PartitionSpec as P


HEAD_SIZE = 128
BLK = 64
GROUP_BLOCKS = 4
ROPE_BASE = 500000.0
NEG = -1e30


def turn_tables(positions):
    half = HEAD_SIZE // 2
    freq = ROPE_BASE ** (-jnp.arange(half, dtype=jnp.float32) / half)
    angle = positions[:, None] * freq[None, :]
    cosine, sine = jnp.cos(angle), jnp.sin(angle)
    return (
        jnp.concatenate([cosine, cosine], axis=1),
        jnp.concatenate([-sine, sine], axis=1),
    )


def fetch_rows(sources, starts, rows, buffer, sem):
    copies = []
    for index, start in enumerate(starts):
        at = 0
        for which, source in enumerate(sources):
            width = source.shape[1]
            copy = pltpu.make_async_copy(
                source.at[pl.ds(pl.multiple_of(start, rows), rows), :],
                buffer.at[index, :, pl.ds(at, width)],
                sem.at[index, which],
            )
            copy.start()
            copies.append(copy)
            at += width
    return copies


def dot(a, b):
    return jnp.dot(a, b, preferred_element_type=jnp.float32)


def near_kernel(spans, starts_ref, own_ref, near_ref, wq, wk, wv, *rest):
    outs, (buffer, sem) = rest[: len(spans)], rest[len(spans) :]
    feat = own_ref.shape[1]
    copies = fetch_rows(
        (wq, wk, wv), (starts_ref[0], starts_ref[1]), feat, buffer, sem
    )
    for copy in copies:
        copy.wait()
    for (a, b), out in zip(spans, outs):
        out[...] = dot(own_ref[a:b], buffer[0]) + dot(near_ref[a:b], buffer[1])


def far_kernel(starts_ref, far_ref, sum_ref, wq, wk, wv, out_ref, buffer, sem):
    feat = far_ref.shape[1]
    for copy in fetch_rows((wq, wk, wv), (starts_ref[2],), feat, buffer, sem):
        copy.wait()
    out_ref[...] = sum_ref[...] + dot(far_ref[...], buffer[0])


def last_kernel(
    starts_ref, far_ref, sum_ref, cos_ref, sin_ref, wq, wk, wv, q_ref, kv_ref, buffer, sem
):
    feat = far_ref.shape[1]
    for copy in fetch_rows((wq, wk, wv), (starts_ref[3],), feat, buffer, sem):
        copy.wait()
    product = sum_ref[...] + dot(far_ref[...], buffer[0])
    cosine, sine = cos_ref[...], sin_ref[...]
    width = q_ref.shape[1]
    for at in range(0, width + HEAD_SIZE, HEAD_SIZE):
        piece = product[:, at : at + HEAD_SIZE]
        turned = piece * cosine + pltpu.roll(piece, HEAD_SIZE // 2, 1) * sine
        if at < width:
            q_ref[:, at : at + HEAD_SIZE] = turned.astype(jnp.bfloat16)
        else:
            kv_ref[:, :HEAD_SIZE] = turned.astype(jnp.bfloat16)
    kv_ref[:, HEAD_SIZE:] = product[:, width + HEAD_SIZE :].astype(jnp.bfloat16)


SMEM = pl.BlockSpec(memory_space=pltpu.SMEM)
VMEM = pl.BlockSpec(memory_space=pltpu.VMEM)
ANY = pl.BlockSpec(memory_space=pl.ANY)
HBM = pl.BlockSpec(memory_space=pltpu.HBM)


def call(kernel, ins, outs, scratch, args, flops, bytes_accessed, aliases=None):
    args = [
        pltpu.with_memory_space_constraint(arg, pltpu.HBM) if spec is HBM else arg
        for spec, arg in zip(ins, args)
    ]
    return pl.pallas_call(
        kernel,
        out_shape=outs,
        in_specs=ins,
        out_specs=jax.tree.map(lambda _: VMEM, outs),
        scratch_shapes=scratch,
        input_output_aliases=aliases or {},
        compiler_params=pltpu.CompilerParams(vmem_limit_bytes=20 << 20),
        cost_estimate=pl.CostEstimate(
            flops=flops, transcendentals=0, bytes_accessed=bytes_accessed
        ),
    )(*args)


def out_kernel(starts_ref, own_ref, partner_ref, wo, partner_w, out_ref, buffer, sem):
    feat = out_ref.shape[1]
    copy = pltpu.make_async_copy(
        wo.at[:, pl.ds(pl.multiple_of(starts_ref[0], feat), feat)], buffer.at[0], sem.at[0]
    )
    other = pltpu.make_async_copy(partner_w, buffer.at[1], sem.at[1])
    copy.start()
    other.start()
    copy.wait()
    other.wait()
    total = dot(own_ref[...], buffer[0]) + dot(partner_ref[...], buffer[1])
    out_ref[...] = total.astype(out_ref.dtype)


def final_kernel(spans, *refs):
    out_ref = refs[-1]
    count = len(spans)
    for (a, b), kept, arrived in zip(spans, refs[:count], refs[count : 2 * count]):
        out_ref[a:b] = (kept[...] + arrived[...].astype(jnp.float32)).astype(
            jnp.bfloat16
        )


def attend_kernel(heads, qblocks, nsel, part_rows, *refs):
    offsets_ref, counts_ref, q_ref = refs[:3]
    parts = refs[3 : 3 + len(part_rows)]
    out_ref, kv_ref, sem = refs[3 + len(part_rows) :]
    at = 0
    copies = []
    for index, (part, rows) in enumerate(zip(parts, part_rows)):
        copy = pltpu.make_async_copy(part, kv_ref.at[pl.ds(at, rows)], sem.at[index])
        copy.start()
        copies.append(copy)
        at += rows
    for copy in copies:
        copy.wait()
    width = GROUP_BLOCKS * BLK
    groups = nsel // GROUP_BLOCKS
    scale = HEAD_SIZE**-0.5

    def one_qblock(qb, carry):
        lane = lax.broadcasted_iota(jnp.int32, (BLK, width), 1)
        row = lax.broadcasted_iota(jnp.int32, (BLK, width), 0)
        rows = pl.ds(pl.multiple_of(qb * BLK, BLK), BLK)
        for head in range(heads):
            columns = slice(head * HEAD_SIZE, (head + 1) * HEAD_SIZE)
            query = q_ref[rows, columns]
            place = head * qblocks + qb
            count = counts_ref[place]
            scores = []
            values = []
            for group in range(groups):
                pieces = []
                for slot in range(GROUP_BLOCKS):
                    start = offsets_ref[place * nsel + group * GROUP_BLOCKS + slot]
                    pieces.append(kv_ref[pl.ds(pl.multiple_of(start, BLK), BLK), :])
                both = jnp.concatenate(pieces, axis=0)
                values.append(both[:, HEAD_SIZE:])
                score = lax.dot_general(
                    query,
                    both[:, :HEAD_SIZE],
                    (((1,), (1,)), ((), ())),
                    preferred_element_type=jnp.float32,
                )
                allowed = lane < (count - group * GROUP_BLOCKS) * BLK
                if group == 0:
                    allowed = allowed & ((lane >= BLK) | (lane <= row))
                scores.append(jnp.where(allowed, score, NEG))
            highest = jnp.max(
                functools.reduce(jnp.maximum, scores), axis=-1, keepdims=True
            )
            total = jnp.zeros((BLK, width), jnp.float32)
            summed = jnp.zeros((BLK, HEAD_SIZE), jnp.float32)
            for score, value in zip(scores, values):
                weights = jnp.exp((score - highest) * scale)
                total = total + weights
                summed = summed + jnp.dot(
                    weights.astype(jnp.bfloat16),
                    value,
                    preferred_element_type=jnp.float32,
                )
            total = jnp.sum(total, axis=-1, keepdims=True)
            out_ref[rows, columns] = (summed / total).astype(jnp.bfloat16)
        return carry

    lax.fori_loop(0, qblocks, one_qblock, 0)


def attend(offsets, counts, query, parts, heads, qblocks, nsel):
    part_rows = tuple(part.shape[0] for part in parts)
    return pl.pallas_call(
        functools.partial(attend_kernel, heads, qblocks, nsel, part_rows),
        out_shape=jax.ShapeDtypeStruct(query.shape, jnp.bfloat16),
        in_specs=[pl.BlockSpec(memory_space=pltpu.SMEM)] * 2
        + [pl.BlockSpec(memory_space=pltpu.VMEM)]
        + [pl.BlockSpec(memory_space=pl.ANY)] * len(parts),
        out_specs=pl.BlockSpec(memory_space=pltpu.VMEM),
        scratch_shapes=[
            pltpu.VMEM((sum(part_rows), 2 * HEAD_SIZE), jnp.bfloat16),
            pltpu.SemaphoreType.DMA((len(parts),)),
        ],
        compiler_params=pltpu.CompilerParams(vmem_limit_bytes=24 << 20),
        cost_estimate=pl.CostEstimate(
            flops=4 * heads * qblocks * nsel * BLK * BLK * HEAD_SIZE,
            transcendentals=heads * qblocks * nsel * BLK * BLK,
            bytes_accessed=sum(part_rows) * 4 * HEAD_SIZE,
        ),
    )(offsets, counts, query, *parts)


def on_device(mesh, tokens, w_query, w_key, w_value, w_out, block_ids, block_counts):
    cols, toks = mesh.shape["col"], mesh.shape["tok"]
    tok_rows, feat = tokens.shape
    heads = w_query.shape[1] // HEAD_SIZE
    qblocks, nsel = block_ids.shape[1:]
    col = lax.axis_index("col")
    tok = lax.axis_index("tok")
    lines = toks // 2
    bf16, f32 = jnp.bfloat16, jnp.float32

    def over_col(value, flip):
        return lax.ppermute(value, "col", [(i, i ^ flip) for i in range(cols)])

    def across(value):
        return lax.ppermute(value, "tok", [(i, i ^ 1) for i in range(toks)])

    def up(value, steps):
        return lax.ppermute(
            value, "tok", [(i, i + 2 * steps) for i in range(toks - 2 * steps)]
        )

    first = (qblocks + 1) // 2 * BLK
    spans = [(0, first), (first, tok_rows)]
    far_parts = []
    for a, b in spans:
        far_parts.append(over_col(tokens[a:b], 2))
    near = over_col(tokens, 1)
    partner_near = over_col(
        lax.dynamic_slice_in_dim(w_out, (col ^ 1) * feat, feat, 1), 1
    )
    partner_far = over_col(
        lax.dynamic_slice_in_dim(w_out, (col ^ 3) * feat, feat, 1), 1
    )

    starts = (col ^ jnp.arange(4, dtype=jnp.int32)) * feat
    ws = (w_query, w_key, w_value)
    width = sum(w.shape[1] for w in ws)

    def weight_scratch(count):
        return [
            pltpu.VMEM((count, feat, width), bf16),
            pltpu.SemaphoreType.DMA((count, len(ws))),
        ]

    sums = call(
        functools.partial(near_kernel, spans),
        [SMEM, VMEM, VMEM, HBM, HBM, HBM],
        [jax.ShapeDtypeStruct((b - a, width), f32) for a, b in spans],
        weight_scratch(2),
        (starts, tokens, near, *ws),
        4 * tok_rows * feat * width,
        4 * feat * width,
    )

    positions = (tok * tok_rows + jnp.arange(tok_rows, dtype=jnp.int32)).astype(f32)
    tables = [turn_tables(positions[a:b]) for a, b in spans]
    live = (
        jnp.arange(nsel, dtype=jnp.int32)[None, None, :] < block_counts[:, :, None]
    )
    chosen = jnp.where(live, block_ids, block_ids[:, :, :1])
    owner, inside = chosen // qblocks, chosen % qblocks
    slot = (tok // 2 - owner // 2) * 2 + ((owner % 2) ^ (tok % 2))
    offsets = slot * tok_rows + inside * BLK

    queries = []
    shards = [[] for _ in range(toks)]
    for (a, b), far, summed, (cosine, sine) in zip(spans, far_parts, sums, tables):
        rows = b - a
        opposite = over_col(far, 1)
        summed = call(
            far_kernel,
            [SMEM, VMEM, VMEM, HBM, HBM, HBM],
            jax.ShapeDtypeStruct((rows, width), f32),
            weight_scratch(1),
            (starts, far, summed, *ws),
            2 * rows * feat * width,
            2 * feat * width,
        )
        query, pair = call(
            last_kernel,
            [SMEM, VMEM, VMEM, VMEM, VMEM, HBM, HBM, HBM],
            [
                jax.ShapeDtypeStruct((rows, heads * HEAD_SIZE), bf16),
                jax.ShapeDtypeStruct((rows, 2 * HEAD_SIZE), bf16),
            ],
            weight_scratch(1),
            (starts, opposite, summed, cosine, sine, *ws),
            2 * rows * feat * width,
            2 * feat * width,
        )
        queries.append(query)
        for line in range(lines):
            moved = pair
            if line:
                moved = up(pair, line)
            shards[2 * line + 1].append(across(moved))
            shards[2 * line].append(moved)
    parts = [piece for shard in shards for piece in shard]

    keeps, arrivals = [], []
    for (a, b), query in zip(spans, queries):
        rows, qa, qb = b - a, a // BLK, b // BLK
        attended = attend(
            offsets[:, qa:qb].reshape(-1),
            block_counts[:, qa:qb].reshape(-1),
            query,
            parts,
            heads,
            qb - qa,
            nsel,
        )
        partner = over_col(attended, 1)

        def project(start, partner_w, kind):
            return call(
                out_kernel,
                [SMEM, VMEM, VMEM, HBM, HBM],
                jax.ShapeDtypeStruct((rows, feat), kind),
                [
                    pltpu.VMEM((2, w_out.shape[0], feat), bf16),
                    pltpu.SemaphoreType.DMA((2,)),
                ],
                (start, attended, partner, w_out, partner_w),
                4 * rows * feat * w_out.shape[0],
                4 * feat * w_out.shape[0],
            )

        sent = project(starts[2:3], partner_far, bf16)
        arrivals.append(over_col(sent, 2))
        keeps.append(project(starts[0:1], partner_near, f32))
    return call(
        functools.partial(final_kernel, spans),
        [VMEM] * (2 * len(spans)),
        jax.ShapeDtypeStruct((tok_rows, feat), bf16),
        [],
        (*keeps, *arrivals),
        tok_rows * feat,
        8 * tok_rows * feat,
    )


def solution(mesh):
    in_specs = (
        P("tok", "col"),
        P(None, "col"),
        P(None, "col"),
        P(None, "col"),
        P("col", None),
        P("col", "tok", None),
        P("col", "tok"),
    )

    def body(*args):
        return on_device(mesh, *args)

    return jax.shard_map(
        body,
        mesh=mesh,
        in_specs=in_specs,
        out_specs=P("tok", "col"),
        check_vma=False,
    )
```

```python
import functools

import jax
import jax.numpy as jnp
from jax import lax
from jax.experimental import pallas as pl
from jax.experimental.pallas import tpu as pltpu
from jax.sharding import PartitionSpec as P


HEAD_SIZE = 128
BLK = 64
GROUP_BLOCKS = 4
ROPE_BASE = 500000.0
NEG = -1e30


SMEM = pl.BlockSpec(memory_space=pltpu.SMEM)
VMEM = pl.BlockSpec(memory_space=pltpu.VMEM)
HBM = pl.BlockSpec(memory_space=pltpu.HBM)

bf16, f32 = jnp.bfloat16, jnp.float32


def shape(dims, kind=bf16):
    return jax.ShapeDtypeStruct(dims, kind)


def call(kernel, ins, outs, args, flops, scratch=(), vmem=10, grown=0):
    args = [
        pltpu.with_memory_space_constraint(arg, pltpu.HBM) if spec is HBM else arg
        for spec, arg in zip(ins, args)
    ]
    moved = sum(x.size * x.dtype.itemsize for x in jax.tree.leaves((outs, args)))
    return pl.pallas_call(
        kernel,
        out_shape=outs,
        in_specs=ins,
        out_specs=jax.tree.map(lambda _: VMEM, outs),
        scratch_shapes=list(scratch),
        compiler_params=pltpu.CompilerParams(vmem_limit_bytes=vmem << 20),
        cost_estimate=pl.CostEstimate(
            flops=flops, transcendentals=grown, bytes_accessed=moved
        ),
    )(*args)


def dot(a, b):
    return jnp.dot(a, b, preferred_element_type=f32)


def turn_tables(positions):
    half = HEAD_SIZE // 2
    freq = ROPE_BASE ** (-jnp.arange(half, dtype=f32) / half)
    angle = positions[:, None] * freq[None, :]
    cosine, sine = jnp.cos(angle), jnp.sin(angle)
    return (
        jnp.concatenate([cosine, cosine], axis=1),
        jnp.concatenate([-sine, sine], axis=1),
    )


def run_copies(pairs, sem):
    copies = [
        pltpu.make_async_copy(source, target, sem.at[index])
        for index, (source, target) in enumerate(pairs)
    ]
    for copy in copies:
        copy.start()
    for copy in copies:
        copy.wait()


def split_kernel(spans, tokens, *rest):
    outs, sem = rest[:-1], rest[-1]
    run_copies(
        [(tokens.at[pl.ds(a, b - a)], out) for (a, b), out in zip(spans, outs)], sem
    )


def columns_kernel(starts_ref, wo, *rest):
    outs, sem = rest[:-1], rest[-1]
    feat = outs[0].shape[1]
    run_copies(
        [
            (wo.at[:, pl.ds(pl.multiple_of(starts_ref[index], feat), feat)], out)
            for index, out in enumerate(outs)
        ],
        sem,
    )


def rows_kernel(starts_ref, *rest):
    sources, outs, sem = rest[:3], rest[3:-1], rest[-1]
    feat = outs[0].shape[0]
    pairs = []
    for index, out in enumerate(outs):
        rows = pl.ds(pl.multiple_of(starts_ref[index], feat), feat)
        at = 0
        for source in sources:
            width = source.shape[1]
            pairs.append((source.at[rows, :], out.at[:, pl.ds(at, width)]))
            at += width
    run_copies(pairs, sem)


def near_kernel(spans, own_ref, near_ref, w0, w1, *outs):
    for (a, b), out in zip(spans, outs):
        out[...] = dot(own_ref[a:b], w0[...]) + dot(near_ref[a:b], w1[...])


def far_kernel(far_ref, sum_ref, w, out_ref):
    out_ref[...] = sum_ref[...] + dot(far_ref[...], w[...])


def last_kernel(a, b, far_ref, sum_ref, cos_ref, sin_ref, w, q_ref, kv_ref):
    product = sum_ref[...] + dot(far_ref[...], w[...])
    cosine, sine = cos_ref[a:b], sin_ref[a:b]
    width = q_ref.shape[1]
    for at in range(0, width + HEAD_SIZE, HEAD_SIZE):
        piece = product[:, at : at + HEAD_SIZE]
        turned = piece * cosine + pltpu.roll(piece, HEAD_SIZE // 2, 1) * sine
        if at < width:
            q_ref[:, at : at + HEAD_SIZE] = turned.astype(bf16)
        else:
            kv_ref[:, :HEAD_SIZE] = turned.astype(bf16)
    kv_ref[:, HEAD_SIZE:] = product[:, width + HEAD_SIZE :].astype(bf16)


def out_kernel(own_ref, partner_ref, own_w, partner_w, out_ref):
    total = dot(own_ref[...], own_w[...]) + dot(partner_ref[...], partner_w[...])
    out_ref[...] = total.astype(out_ref.dtype)


def final_kernel(spans, *refs):
    out_ref = refs[-1]
    count = len(spans)
    for (a, b), kept, arrived in zip(spans, refs[:count], refs[count : 2 * count]):
        out_ref[a:b] = (kept[...] + arrived[...].astype(f32)).astype(bf16)


def attend_kernel(heads, qblocks, nsel, count, *refs):
    offsets_ref, counts_ref, q_ref = refs[:3]
    parts = refs[3 : 3 + count]
    out_ref, kv_ref = refs[3 + count :]
    at = 0
    for part in parts:
        kv_ref[at : at + part.shape[0]] = part[...]
        at += part.shape[0]
    width = GROUP_BLOCKS * BLK
    groups = nsel // GROUP_BLOCKS
    scale = HEAD_SIZE**-0.5

    def one_qblock(qb, carry):
        lane = lax.broadcasted_iota(jnp.int32, (BLK, width), 1)
        row = lax.broadcasted_iota(jnp.int32, (BLK, width), 0)
        rows = pl.ds(pl.multiple_of(qb * BLK, BLK), BLK)
        for head in range(heads):
            columns = slice(head * HEAD_SIZE, (head + 1) * HEAD_SIZE)
            query = q_ref[rows, columns]
            place = head * qblocks[2] + qblocks[0] + qb
            live = counts_ref[place]
            scores = []
            values = []
            for group in range(groups):
                pieces = []
                for slot in range(GROUP_BLOCKS):
                    start = offsets_ref[place * nsel + group * GROUP_BLOCKS + slot]
                    pieces.append(kv_ref[pl.ds(pl.multiple_of(start, BLK), BLK), :])
                both = jnp.concatenate(pieces, axis=0)
                values.append(both[:, HEAD_SIZE:])
                score = lax.dot_general(
                    query,
                    both[:, :HEAD_SIZE],
                    (((1,), (1,)), ((), ())),
                    preferred_element_type=f32,
                )
                allowed = lane < (live - group * GROUP_BLOCKS) * BLK
                if group == 0:
                    allowed = allowed & ((lane >= BLK) | (lane <= row))
                scores.append(jnp.where(allowed, score, NEG))
            highest = jnp.max(
                functools.reduce(jnp.maximum, scores), axis=-1, keepdims=True
            )
            total = jnp.zeros((BLK, width), f32)
            summed = jnp.zeros((BLK, HEAD_SIZE), f32)
            for score, value in zip(scores, values):
                weights = jnp.exp((score - highest) * scale)
                total = total + weights
                summed = summed + dot(weights.astype(bf16), value)
            total = jnp.sum(total, axis=-1, keepdims=True)
            out_ref[rows, columns] = (summed / total).astype(bf16)
        return carry

    lax.fori_loop(0, qblocks[1] - qblocks[0], one_qblock, 0)


def attend(offsets, counts, query, parts, heads, qblocks, nsel):
    pairs = query.size // HEAD_SIZE * nsel * BLK
    held = sum(part.size for part in parts) * 2 >> 20
    return call(
        functools.partial(attend_kernel, heads, qblocks, nsel, len(parts)),
        [SMEM, SMEM, VMEM] + [VMEM] * len(parts),
        shape(query.shape),
        (offsets, counts, query, *parts),
        4 * pairs * HEAD_SIZE,
        scratch=[pltpu.VMEM((sum(p.shape[0] for p in parts), 2 * HEAD_SIZE), bf16)],
        vmem=8 + 3 * held,
        grown=pairs,
    )


def on_device(mesh, tokens, w_query, w_key, w_value, w_out, block_ids, block_counts):
    cols, toks = mesh.shape["col"], mesh.shape["tok"]
    tok_rows, feat = tokens.shape
    heads = w_query.shape[1] // HEAD_SIZE
    qblocks, nsel = block_ids.shape[1:]
    col = lax.axis_index("col")
    tok = lax.axis_index("tok")
    lines = toks // 2
    inner = w_out.shape[0]
    ws = (w_query, w_key, w_value)
    width = sum(w.shape[1] for w in ws)

    def over_col(value, flip):
        return lax.ppermute(value, "col", [(i, i ^ flip) for i in range(cols)])

    def across(value):
        return lax.ppermute(value, "tok", [(i, i ^ 1) for i in range(toks)])

    def up(value, steps):
        return lax.ppermute(
            value, "tok", [(i, (i + 2 * steps) % toks) for i in range(toks)]
        )

    first = (qblocks + 1) // 2 * BLK
    spans = [(0, first), (first, tok_rows)]
    starts = (col ^ jnp.arange(4, dtype=jnp.int32)) * feat
    pieces = call(
        functools.partial(split_kernel, spans),
        [HBM],
        [shape((b - a, feat)) for a, b in spans],
        (tokens,),
        0,
        scratch=[pltpu.SemaphoreType.DMA((len(spans),))],
    )
    far_parts = []
    for piece in pieces:
        far_parts.append(over_col(piece, 2))
    near = over_col(tokens, 1)
    block_ids, block_counts, _ = lax.optimization_barrier(
        (block_ids, block_counts, pieces[0])
    )
    positions = (tok * tok_rows + jnp.arange(tok_rows, dtype=jnp.int32)).astype(f32)
    cosine, sine = turn_tables(positions)
    live = jnp.arange(nsel, dtype=jnp.int32)[None, None, :] < block_counts[:, :, None]
    owner, inside = block_ids // qblocks, block_ids % qblocks
    slot = (tok // 2 - owner // 2) * 2 + ((owner % 2) ^ (tok % 2))
    own = jnp.arange(qblocks, dtype=jnp.int32)[None, :, None] * BLK
    offsets = jnp.where(live, slot * tok_rows + inside * BLK, own).reshape(-1)
    counts = block_counts.reshape(-1)
    starts, cosine, sine, offsets, counts = lax.optimization_barrier(
        (starts, cosine, sine, offsets, counts)
    )
    out_own_near, out_send_near, out_own_far, out_send_far = call(
        columns_kernel,
        [SMEM, HBM],
        [shape((inner, feat))] * 4,
        (starts, w_out),
        0,
        scratch=[pltpu.SemaphoreType.DMA((4,))],
    )
    partner_near = over_col(out_send_near, 1)
    partner_far = over_col(out_send_far, 1)
    weights = call(
        rows_kernel,
        [SMEM, HBM, HBM, HBM],
        [shape((feat, width))] * 4,
        (starts, *ws),
        0,
        scratch=[pltpu.SemaphoreType.DMA((12,))],
    )
    sums = call(
        functools.partial(near_kernel, spans),
        [VMEM] * 4,
        [shape((b - a, width), f32) for a, b in spans],
        (tokens, near, weights[0], weights[1]),
        4 * tok_rows * feat * width,
    )

    queries = []
    shards = [[] for _ in range(toks)]
    for (a, b), far, summed in zip(spans, far_parts, sums):
        rows = b - a
        opposite = over_col(far, 1)
        summed = call(
            far_kernel,
            [VMEM] * 3,
            shape((rows, width), f32),
            (far, summed, weights[2]),
            2 * rows * feat * width,
        )
        query, pair = call(
            functools.partial(last_kernel, a, b),
            [VMEM] * 5,
            [shape((rows, heads * HEAD_SIZE)), shape((rows, 2 * HEAD_SIZE))],
            (opposite, summed, cosine, sine, weights[3]),
            2 * rows * feat * width,
        )
        queries.append(query)
        for line in range(lines):
            moved = pair
            if line:
                moved = up(pair, line)
            shards[2 * line + 1].append(across(moved))
            shards[2 * line].append(moved)
    parts = [piece for shard in shards for piece in shard]

    keeps, arrivals = [], []
    for (a, b), query in zip(spans, queries):
        rows, qa, qb = b - a, a // BLK, b // BLK
        attended = attend(offsets, counts, query, parts, heads, (qa, qb, qblocks), nsel)
        partner = over_col(attended, 1)

        def project(own_w, partner_w, kind):
            return call(
                out_kernel,
                [VMEM] * 4,
                shape((rows, feat), kind),
                (attended, partner, own_w, partner_w),
                4 * rows * feat * inner,
            )

        sent = project(out_own_far, partner_far, bf16)
        arrivals.append(over_col(sent, 2))
        keeps.append(project(out_own_near, partner_near, f32))
    return call(
        functools.partial(final_kernel, spans),
        [VMEM] * (2 * len(spans)),
        shape((tok_rows, feat)),
        (*keeps, *arrivals),
        tok_rows * feat,
    )


def solution(mesh):
    in_specs = (
        P("tok", "col"),
        P(None, "col"),
        P(None, "col"),
        P(None, "col"),
        P("col", None),
        P("col", "tok", None),
        P("col", "tok"),
    )

    def body(*args):
        return on_device(mesh, *args)

    return jax.shard_map(
        body,
        mesh=mesh,
        in_specs=in_specs,
        out_specs=P("tok", "col"),
        check_vma=False,
    )
```

```python
import functools
import math

import jax
import jax.numpy as jnp
from jax import lax
from jax.experimental import pallas as pl
from jax.experimental.pallas import tpu as pltpu
from jax.sharding import PartitionSpec as P


HEAD_SIZE = 128
BLK = 64
GROUP_BLOCKS = 4
ROPE_BASE = 500000.0
NEG = -1e30
CODE = 256


SMEM = pl.BlockSpec(memory_space=pltpu.SMEM)
VMEM = pl.BlockSpec(memory_space=pltpu.VMEM)
HBM = pl.BlockSpec(memory_space=pltpu.HBM)

bf16, f32 = jnp.bfloat16, jnp.float32


def shape(dims, kind=bf16):
    return jax.ShapeDtypeStruct(dims, kind)


def call(kernel, ins, outs, args, flops, scratch=(), vmem=10, grown=0):
    args = [
        pltpu.with_memory_space_constraint(arg, pltpu.HBM) if spec is HBM else arg
        for spec, arg in zip(ins, args)
    ]
    moved = sum(x.size * x.dtype.itemsize for x in jax.tree.leaves((outs, args)))
    return pl.pallas_call(
        kernel,
        out_shape=outs,
        in_specs=ins,
        out_specs=jax.tree.map(lambda x: SMEM if x.dtype == jnp.int32 else VMEM, outs),
        scratch_shapes=list(scratch),
        compiler_params=pltpu.CompilerParams(vmem_limit_bytes=vmem << 20),
        cost_estimate=pl.CostEstimate(
            flops=flops, transcendentals=grown, bytes_accessed=moved
        ),
    )(*args)


def dot(a, b):
    return jnp.dot(a, b, preferred_element_type=f32)


def turn_tables(positions):
    half = HEAD_SIZE // 2
    freq = ROPE_BASE ** (-jnp.arange(half, dtype=f32) / half)
    angle = positions[:, None] * freq[None, :]
    cosine, sine = jnp.cos(angle), jnp.sin(angle)
    return (
        jnp.concatenate([cosine, cosine], axis=1),
        jnp.concatenate([-sine, sine], axis=1),
    )


def run_copies(pairs, sem, meanwhile=lambda: None):
    copies = [
        pltpu.make_async_copy(source, target, sem.at[index])
        for index, (source, target) in enumerate(pairs)
    ]
    for copy in copies:
        copy.start()
    meanwhile()
    for copy in copies:
        copy.wait()


def split_kernel(spans, tokens, *rest):
    outs, sem = rest[:-1], rest[-1]
    run_copies(
        [(tokens.at[pl.ds(a, b - a)], out) for (a, b), out in zip(spans, outs)], sem
    )


def columns_kernel(starts_ref, wo, *rest):
    outs, sem = rest[:-1], rest[-1]
    feat = outs[0].shape[1]
    run_copies(
        [
            (wo.at[:, pl.ds(pl.multiple_of(starts_ref[index], feat), feat)], out)
            for index, out in enumerate(outs)
        ],
        sem,
    )


def sort_rows(counts_ref, order_ref, heads, qblocks, cuts, groups):
    for first, last in cuts:
        at = jnp.int32(first * heads)
        for wanted in range(groups, 0, -1):
            for head in range(heads):
                for block in range(first, last):
                    live = counts_ref[head * qblocks + block]
                    order_ref[at] = jnp.int32(head * CODE + block)
                    needed = (live + GROUP_BLOCKS - 1) // GROUP_BLOCKS
                    at = at + (needed == wanted).astype(jnp.int32)


def rows_kernel(sorting, starts_ref, counts_ref, *rest):
    sources, outs, order_ref, sem = rest[:3], rest[3:-2], rest[-2], rest[-1]
    feat = outs[0].shape[0]
    pairs = []
    for index, out in enumerate(outs):
        rows = pl.ds(pl.multiple_of(starts_ref[index], feat), feat)
        at = 0
        for source in sources:
            width = source.shape[1]
            pairs.append((source.at[rows, :], out.at[:, pl.ds(at, width)]))
            at += width
    run_copies(pairs, sem, lambda: sort_rows(counts_ref, order_ref, *sorting))


def near_kernel(spans, own_ref, near_ref, w0, w1, *outs):
    for (a, b), out in zip(spans, outs):
        out[...] = dot(own_ref[a:b], w0[...]) + dot(near_ref[a:b], w1[...])


def far_kernel(far_ref, sum_ref, w, out_ref):
    out_ref[...] = sum_ref[...] + dot(far_ref[...], w[...])


def last_kernel(a, b, far_ref, sum_ref, cos_ref, sin_ref, w, q_ref, kv_ref):
    product = sum_ref[...] + dot(far_ref[...], w[...])
    cosine, sine = cos_ref[a:b], sin_ref[a:b]
    width = q_ref.shape[1]
    for at in range(0, width + HEAD_SIZE, HEAD_SIZE):
        piece = product[:, at : at + HEAD_SIZE]
        turned = piece * cosine + pltpu.roll(piece, HEAD_SIZE // 2, 1) * sine
        if at < width:
            turned = turned * (HEAD_SIZE**-0.5 * math.log2(math.e))
            q_ref[:, at : at + HEAD_SIZE] = turned.astype(bf16)
        else:
            kv_ref[:, :HEAD_SIZE] = turned.astype(bf16)
    kv_ref[:, HEAD_SIZE:] = product[:, width + HEAD_SIZE :].astype(bf16)


def out_kernel(own_ref, partner_ref, own_w, partner_w, out_ref):
    total = dot(own_ref[...], own_w[...]) + dot(partner_ref[...], partner_w[...])
    out_ref[...] = total.astype(out_ref.dtype)


def final_kernel(spans, *refs):
    out_ref = refs[-1]
    count = len(spans)
    for (a, b), kept, arrived in zip(spans, refs[:count], refs[count : 2 * count]):
        out_ref[a:b] = (kept[...] + arrived[...].astype(f32)).astype(bf16)


def attend_kernel(heads, place, nsel, spans, fresh, count, *refs):
    first, last, qblocks = place
    offsets_ref, counts_ref, order_ref = refs[:3]
    queries, parts = refs[3 : 3 + len(spans)], refs[3 + len(spans) : 3 + count]
    if fresh:
        out_ref, kv_ref, q_ref, o_ref = refs[3 + count :]
        at = 0
        for part in parts:
            kv_ref[at : at + part.shape[0]] = part[...]
            at += part.shape[0]
    else:
        out_ref, q_ref, o_ref = refs[3 + count :]
        (kv_ref,) = parts
    for head in range(heads):
        columns = slice(head * HEAD_SIZE, (head + 1) * HEAD_SIZE)
        for (a, b), part in zip(spans, queries):
            q_ref[head, a:b] = part[:, columns]
    width = GROUP_BLOCKS * BLK

    def some_rows(start, groups):
        lane = lax.broadcasted_iota(jnp.int32, (BLK, width), 1)
        row = lax.broadcasted_iota(jnp.int32, (BLK, width), 0)
        causal = (lane >= BLK) | (lane <= row)
        ones = jnp.ones((groups * width, HEAD_SIZE), bf16)
        places, scores, values = [], [], []
        for member in range(heads):
            code = order_ref[start + member]
            head, block = code // CODE, code % CODE
            index = head * qblocks + block
            query = q_ref[head, pl.ds(pl.multiple_of(block * BLK, BLK), BLK)]
            live = counts_ref[index]
            places.append((head, block))
            scores.append([])
            values.append([])
            for group in range(groups):
                pieces = []
                for slot in range(GROUP_BLOCKS):
                    at = offsets_ref[index * nsel + group * GROUP_BLOCKS + slot]
                    pieces.append(kv_ref[pl.ds(pl.multiple_of(at, BLK), BLK), :])
                both = jnp.concatenate(pieces, axis=0)
                values[-1].append(both[:, HEAD_SIZE:])
                score = lax.dot_general(
                    query,
                    both[:, :HEAD_SIZE],
                    (((1,), (1,)), ((), ())),
                    preferred_element_type=f32,
                )
                allowed = lane < (live - group * GROUP_BLOCKS) * BLK
                if group == 0:
                    allowed = allowed & causal
                scores[-1].append(jnp.where(allowed, score, NEG))
        highest = [
            jnp.max(functools.reduce(jnp.maximum, score), axis=-1, keepdims=True)
            for score in scores
        ]
        for (head, block), score, high, value in zip(places, scores, highest, values):
            weights = jnp.concatenate(
                [jnp.exp2(piece - high).astype(bf16) for piece in score], axis=1
            )
            both = dot(
                weights, jnp.concatenate([jnp.concatenate(value, axis=0), ones], axis=1)
            )
            target = pl.ds(pl.multiple_of((block - first) * BLK, BLK), BLK)
            o_ref[head, target] = (both[:, :HEAD_SIZE] / both[:, HEAD_SIZE:]).astype(bf16)

    def one_batch(batch, carry):
        start = first * heads + batch * heads
        code = order_ref[start]
        live = counts_ref[code // CODE * qblocks + code % CODE]
        needed = (live + GROUP_BLOCKS - 1) // GROUP_BLOCKS
        for groups in range(1, nsel // GROUP_BLOCKS + 1):

            @pl.when(needed == groups)
            def _(groups=groups):
                some_rows(start, groups)

        return carry

    lax.fori_loop(0, last - first, one_batch, 0)
    for head in range(heads):
        out_ref[:, head * HEAD_SIZE : (head + 1) * HEAD_SIZE] = o_ref[head]


def attend(lists, queries, parts, place, nsel, spans, fresh):
    heads = queries[0].shape[1] // HEAD_SIZE
    first, last, _ = place
    rows = (last - first) * BLK
    whole = spans[-1][1]
    keys = sum(part.shape[0] for part in parts)
    held = keys * HEAD_SIZE * 4 >> 20
    out = shape((rows, heads * HEAD_SIZE))
    pairs = rows * heads * nsel * BLK
    return call(
        functools.partial(
            attend_kernel, heads, place, nsel, spans, fresh, len(queries) + len(parts)
        ),
        [SMEM] * len(lists) + [VMEM] * (len(queries) + len(parts)),
        [out, shape((keys, 2 * HEAD_SIZE))] if fresh else out,
        (*lists, *queries, *parts),
        4 * pairs * HEAD_SIZE,
        scratch=[
            pltpu.VMEM((heads, whole, HEAD_SIZE), bf16),
            pltpu.VMEM((heads, rows, HEAD_SIZE), bf16),
        ],
        vmem=8 + 3 * held,
        grown=pairs,
    )


def on_device(mesh, tokens, w_query, w_key, w_value, w_out, block_ids, block_counts):
    cols, toks = mesh.shape["col"], mesh.shape["tok"]
    tok_rows, feat = tokens.shape
    heads = w_query.shape[1] // HEAD_SIZE
    qblocks, nsel = block_ids.shape[1:]
    col = lax.axis_index("col")
    tok = lax.axis_index("tok")
    lines = toks // 2
    inner = w_out.shape[0]
    ws = (w_query, w_key, w_value)
    width = sum(w.shape[1] for w in ws)

    def over_col(value, flip):
        return lax.ppermute(value, "col", [(i, i ^ flip) for i in range(cols)])

    def across(value):
        return lax.ppermute(value, "tok", [(i, i ^ 1) for i in range(toks)])

    def up(value, steps):
        return lax.ppermute(
            value, "tok", [(i, (i + 2 * steps) % toks) for i in range(toks)]
        )

    first = (qblocks + 1) // 2 * BLK
    spans = [(0, first), (first, tok_rows)]
    cuts = [(0, qblocks // 2), (qblocks // 2, qblocks)]
    starts = (col ^ jnp.arange(4, dtype=jnp.int32)) * feat
    pieces = call(
        functools.partial(split_kernel, spans),
        [HBM],
        [shape((b - a, feat)) for a, b in spans],
        (tokens,),
        0,
        scratch=[pltpu.SemaphoreType.DMA((len(spans),))],
    )
    far_parts = []
    for piece in pieces:
        far_parts.append(over_col(piece, 2))
    near = over_col(tokens, 1)
    block_ids, block_counts, _ = lax.optimization_barrier(
        (block_ids, block_counts, pieces[0])
    )
    positions = (tok * tok_rows + jnp.arange(tok_rows, dtype=jnp.int32)).astype(f32)
    cosine, sine = turn_tables(positions)
    live = jnp.arange(nsel, dtype=jnp.int32)[None, None, :] < block_counts[:, :, None]
    owner, inside = block_ids // qblocks, block_ids % qblocks
    slot = (tok // 2 - owner // 2) * 2 + ((owner % 2) ^ (tok % 2))
    own = jnp.arange(qblocks, dtype=jnp.int32)[None, :, None] * BLK
    offsets = jnp.where(live, slot * tok_rows + inside * BLK, own).reshape(-1)
    counts = block_counts.reshape(-1)
    starts, cosine, sine, offsets, counts = lax.optimization_barrier(
        (starts, cosine, sine, offsets, counts)
    )
    out_own_near, out_send_near, out_own_far, out_send_far = call(
        columns_kernel,
        [SMEM, HBM],
        [shape((inner, feat))] * 4,
        (starts, w_out),
        0,
        scratch=[pltpu.SemaphoreType.DMA((4,))],
    )
    partner_near = over_col(out_send_near, 1)
    partner_far = over_col(out_send_far, 1)
    *weights, order = call(
        functools.partial(rows_kernel, (heads, qblocks, cuts, nsel // GROUP_BLOCKS)),
        [SMEM, SMEM, HBM, HBM, HBM],
        [shape((feat, width))] * 4 + [shape((heads * qblocks + 1,), jnp.int32)],
        (starts, counts, *ws),
        0,
        scratch=[pltpu.SemaphoreType.DMA((12,))],
    )
    sums = call(
        functools.partial(near_kernel, spans),
        [VMEM] * 4,
        [shape((b - a, width), f32) for a, b in spans],
        (tokens, near, weights[0], weights[1]),
        4 * tok_rows * feat * width,
    )

    queries = []
    shards = [[] for _ in range(toks)]
    for (a, b), far, summed in zip(spans, far_parts, sums):
        rows = b - a
        opposite = over_col(far, 1)
        summed = call(
            far_kernel,
            [VMEM] * 3,
            shape((rows, width), f32),
            (far, summed, weights[2]),
            2 * rows * feat * width,
        )
        query, pair = call(
            functools.partial(last_kernel, a, b),
            [VMEM] * 5,
            [shape((rows, heads * HEAD_SIZE)), shape((rows, 2 * HEAD_SIZE))],
            (opposite, summed, cosine, sine, weights[3]),
            2 * rows * feat * width,
        )
        queries.append(query)
        for line in range(lines):
            moved = pair
            if line:
                moved = up(pair, line)
            shards[2 * line + 1].append(across(moved))
            shards[2 * line].append(moved)
    parts = [piece for shard in shards for piece in shard]

    keeps, arrivals = [], []
    lists = (offsets, counts, order)
    out_spans = [(first * BLK, last * BLK) for first, last in cuts]
    for part, (first, last) in enumerate(cuts):
        rows = (last - first) * BLK
        attended = attend(
            lists, queries, parts, (first, last, qblocks), nsel, spans, part == 0
        )
        if part == 0:
            attended, gathered = attended
            parts = [gathered]
        partner = over_col(attended, 1)

        def project(own_w, partner_w, kind):
            return call(
                out_kernel,
                [VMEM] * 4,
                shape((rows, feat), kind),
                (attended, partner, own_w, partner_w),
                4 * rows * feat * inner,
            )

        sent = project(out_own_far, partner_far, bf16)
        arrivals.append(over_col(sent, 2))
        keeps.append(project(out_own_near, partner_near, f32))
    return call(
        functools.partial(final_kernel, out_spans),
        [VMEM] * (2 * len(out_spans)),
        shape((tok_rows, feat)),
        (*keeps, *arrivals),
        tok_rows * feat,
    )


def solution(mesh):
    in_specs = (
        P("tok", "col"),
        P(None, "col"),
        P(None, "col"),
        P(None, "col"),
        P("col", None),
        P("col", "tok", None),
        P("col", "tok"),
    )

    def body(*args):
        return on_device(mesh, *args)

    return jax.shard_map(
        body,
        mesh=mesh,
        in_specs=in_specs,
        out_specs=P("tok", "col"),
        check_vma=False,
    )
```

```python
import functools
import math

import jax
import jax.numpy as jnp
from jax import lax
from jax.experimental import pallas as pl
from jax.experimental.pallas import tpu as pltpu
from jax.sharding import PartitionSpec as P


HEAD_SIZE = 128
BLK = 64
GROUP_BLOCKS = 4
ROPE_BASE = 500000.0
NEG = -1e30
CODE = 256


SMEM = pl.BlockSpec(memory_space=pltpu.SMEM)
VMEM = pl.BlockSpec(memory_space=pltpu.VMEM)
HBM = pl.BlockSpec(memory_space=pltpu.HBM)

bf16, f32 = jnp.bfloat16, jnp.float32


def shape(dims, kind=bf16):
    return jax.ShapeDtypeStruct(dims, kind)


def call(kernel, ins, outs, args, flops, scratch=(), vmem=10, grown=0):
    args = [
        pltpu.with_memory_space_constraint(arg, pltpu.HBM) if spec is HBM else arg
        for spec, arg in zip(ins, args)
    ]
    moved = sum(x.size * x.dtype.itemsize for x in jax.tree.leaves((outs, args)))
    return pl.pallas_call(
        kernel,
        out_shape=outs,
        in_specs=ins,
        out_specs=jax.tree.map(lambda x: SMEM if x.dtype == jnp.int32 else VMEM, outs),
        scratch_shapes=list(scratch),
        compiler_params=pltpu.CompilerParams(vmem_limit_bytes=vmem << 20),
        cost_estimate=pl.CostEstimate(
            flops=flops, transcendentals=grown, bytes_accessed=moved
        ),
    )(*args)


def dot(a, b):
    return jnp.dot(a, b, preferred_element_type=f32)


def turn_tables(positions):
    half = HEAD_SIZE // 2
    freq = ROPE_BASE ** (-jnp.arange(half, dtype=f32) / half)
    angle = positions[:, None] * freq[None, :]
    cosine, sine = jnp.cos(angle), jnp.sin(angle)
    return (
        jnp.concatenate([cosine, cosine], axis=1),
        jnp.concatenate([-sine, sine], axis=1),
    )


def run_copies(pairs, sem, meanwhile=lambda: None):
    copies = [
        pltpu.make_async_copy(source, target, sem.at[index])
        for index, (source, target) in enumerate(pairs)
    ]
    for copy in copies:
        copy.start()
    meanwhile()
    for copy in copies:
        copy.wait()


def split_kernel(spans, tokens, *rest):
    outs, sem = rest[:-1], rest[-1]
    run_copies(
        [(tokens.at[pl.ds(a, b - a)], out) for (a, b), out in zip(spans, outs)], sem
    )


def columns_kernel(starts_ref, wo, *rest):
    outs, sem = rest[:-1], rest[-1]
    feat = outs[0].shape[1]
    run_copies(
        [
            (wo.at[:, pl.ds(pl.multiple_of(starts_ref[index], feat), feat)], out)
            for index, out in enumerate(outs)
        ],
        sem,
    )


def sort_rows(counts_ref, order_ref, heads, qblocks, cuts, groups):
    for first, last in cuts:
        members = [(head, block) for head in range(heads) for block in range(first, last)]
        needed = [
            (counts_ref[head * qblocks + block] + GROUP_BLOCKS - 1) // GROUP_BLOCKS
            for head, block in members
        ]
        at = jnp.int32(first * heads)
        for wanted in range(groups, 0, -1):
            for (head, block), need in zip(members, needed):
                order_ref[at] = jnp.int32(head * CODE + block)
                at = at + (need == wanted).astype(jnp.int32)


def rows_kernel(sorting, starts_ref, counts_ref, *rest):
    sources, outs, order_ref, sem = rest[:3], rest[3:-2], rest[-2], rest[-1]
    feat = outs[0].shape[0]
    pairs = []
    for index, out in enumerate(outs):
        rows = pl.ds(pl.multiple_of(starts_ref[index], feat), feat)
        at = 0
        for source in sources:
            width = source.shape[1]
            pairs.append((source.at[rows, :], out.at[:, pl.ds(at, width)]))
            at += width
    run_copies(pairs, sem, lambda: sort_rows(counts_ref, order_ref, *sorting))


def near_kernel(spans, own_ref, near_ref, w0, w1, *outs):
    for (a, b), out in zip(spans, outs):
        out[...] = dot(own_ref[a:b], w0[...]) + dot(near_ref[a:b], w1[...])


def far_kernel(far_ref, sum_ref, w, out_ref):
    out_ref[...] = sum_ref[...] + dot(far_ref[...], w[...])


def last_kernel(a, b, far_ref, sum_ref, cos_ref, sin_ref, w, q_ref, kv_ref):
    product = sum_ref[...] + dot(far_ref[...], w[...])
    cosine, sine = cos_ref[a:b], sin_ref[a:b]
    width = q_ref.shape[1]
    for at in range(0, width + HEAD_SIZE, HEAD_SIZE):
        piece = product[:, at : at + HEAD_SIZE]
        turned = piece * cosine + pltpu.roll(piece, HEAD_SIZE // 2, 1) * sine
        if at < width:
            turned = turned * (HEAD_SIZE**-0.5 * math.log2(math.e))
            q_ref[:, at : at + HEAD_SIZE] = turned.astype(bf16)
        else:
            kv_ref[:, :HEAD_SIZE] = turned.astype(bf16)
    kv_ref[:, HEAD_SIZE:] = product[:, width + HEAD_SIZE :].astype(bf16)


def out_kernel(own_ref, partner_ref, own_w, partner_w, out_ref):
    total = dot(own_ref[...], own_w[...]) + dot(partner_ref[...], partner_w[...])
    out_ref[...] = total.astype(out_ref.dtype)


def final_kernel(spans, *refs):
    out_ref = refs[-1]
    count = len(spans)
    for (a, b), kept, arrived in zip(spans, refs[:count], refs[count : 2 * count]):
        out_ref[a:b] = (kept[...] + arrived[...].astype(f32)).astype(bf16)


def attend_kernel(heads, place, nsel, spans, fresh, count, *refs):
    first, last, qblocks = place
    offsets_ref, counts_ref, order_ref = refs[:3]
    queries, parts = refs[3 : 3 + len(spans)], refs[3 + len(spans) : 3 + count]
    if fresh:
        out_ref, kv_ref, q_ref, o_ref = refs[3 + count :]
        at = 0
        for part in parts:
            kv_ref[at : at + part.shape[0]] = part[...]
            at += part.shape[0]
    else:
        out_ref, q_ref, o_ref = refs[3 + count :]
        (kv_ref,) = parts
    for head in range(heads):
        columns = slice(head * HEAD_SIZE, (head + 1) * HEAD_SIZE)
        for (a, b), part in zip(spans, queries):
            q_ref[head, a:b] = part[:, columns]
    width = GROUP_BLOCKS * BLK

    def some_rows(start, groups):
        lane = lax.broadcasted_iota(jnp.int32, (BLK, width), 1)
        row = lax.broadcasted_iota(jnp.int32, (BLK, width), 0)
        causal = (lane >= BLK) | (lane <= row)
        ones = jnp.ones((groups * width, HEAD_SIZE), bf16)
        places, scores, values = [], [], []
        for member in range(heads):
            code = order_ref[start + member]
            head, block = code // CODE, code % CODE
            index = head * qblocks + block
            query = q_ref[head, pl.ds(pl.multiple_of(block * BLK, BLK), BLK)]
            live = counts_ref[index]
            places.append((head, block))
            scores.append([])
            values.append([])
            for group in range(groups):
                pieces = []
                for slot in range(GROUP_BLOCKS):
                    at = offsets_ref[index * nsel + group * GROUP_BLOCKS + slot]
                    pieces.append(kv_ref[pl.ds(pl.multiple_of(at, BLK), BLK), :])
                both = jnp.concatenate(pieces, axis=0)
                values[-1].append(both[:, HEAD_SIZE:])
                score = lax.dot_general(
                    query,
                    both[:, :HEAD_SIZE],
                    (((1,), (1,)), ((), ())),
                    preferred_element_type=f32,
                )
                allowed = lane < (live - group * GROUP_BLOCKS) * BLK
                if group == 0:
                    allowed = allowed & causal
                scores[-1].append(jnp.where(allowed, score, NEG))
        highest = [
            jnp.max(functools.reduce(jnp.maximum, score), axis=-1, keepdims=True)
            for score in scores
        ]
        for (head, block), score, high, value in zip(places, scores, highest, values):
            weights = jnp.concatenate(
                [jnp.exp2(piece - high).astype(bf16) for piece in score], axis=1
            )
            both = dot(
                weights, jnp.concatenate([jnp.concatenate(value, axis=0), ones], axis=1)
            )
            target = pl.ds(pl.multiple_of((block - first) * BLK, BLK), BLK)
            o_ref[head, target] = (both[:, :HEAD_SIZE] / both[:, HEAD_SIZE:]).astype(bf16)

    def one_batch(batch, carry):
        start = first * heads + batch * heads
        code = order_ref[start]
        live = counts_ref[code // CODE * qblocks + code % CODE]
        needed = (live + GROUP_BLOCKS - 1) // GROUP_BLOCKS
        for groups in range(1, nsel // GROUP_BLOCKS + 1):

            @pl.when(needed == groups)
            def _(groups=groups):
                some_rows(start, groups)

        return carry

    lax.fori_loop(0, last - first, one_batch, 0)
    for head in range(heads):
        out_ref[:, head * HEAD_SIZE : (head + 1) * HEAD_SIZE] = o_ref[head]


def attend(lists, queries, parts, place, nsel, spans, fresh):
    heads = queries[0].shape[1] // HEAD_SIZE
    first, last, _ = place
    rows = (last - first) * BLK
    whole = spans[-1][1]
    keys = sum(part.shape[0] for part in parts)
    held = keys * HEAD_SIZE * 4 >> 20
    out = shape((rows, heads * HEAD_SIZE))
    pairs = rows * heads * nsel * BLK
    return call(
        functools.partial(
            attend_kernel, heads, place, nsel, spans, fresh, len(queries) + len(parts)
        ),
        [SMEM] * len(lists) + [VMEM] * (len(queries) + len(parts)),
        [out, shape((keys, 2 * HEAD_SIZE))] if fresh else out,
        (*lists, *queries, *parts),
        4 * pairs * HEAD_SIZE,
        scratch=[
            pltpu.VMEM((heads, whole, HEAD_SIZE), bf16),
            pltpu.VMEM((heads, rows, HEAD_SIZE), bf16),
        ],
        vmem=8 + 3 * held,
        grown=pairs,
    )


def on_device(mesh, tokens, w_query, w_key, w_value, w_out, block_ids, block_counts):
    cols, toks = mesh.shape["col"], mesh.shape["tok"]
    tok_rows, feat = tokens.shape
    heads = w_query.shape[1] // HEAD_SIZE
    qblocks, nsel = block_ids.shape[1:]
    col = lax.axis_index("col")
    tok = lax.axis_index("tok")
    lines = toks // 2
    inner = w_out.shape[0]
    ws = (w_query, w_key, w_value)
    width = sum(w.shape[1] for w in ws)

    def over_col(value, flip):
        return lax.ppermute(value, "col", [(i, i ^ flip) for i in range(cols)])

    def across(value):
        return lax.ppermute(value, "tok", [(i, i ^ 1) for i in range(toks)])

    def up(value, steps):
        return lax.ppermute(
            value, "tok", [(i, (i + 2 * steps) % toks) for i in range(toks)]
        )

    first = (qblocks + 1) // 2 * BLK
    spans = [(0, first), (first, tok_rows)]
    cuts = [(0, qblocks // 2), (qblocks // 2, qblocks)]
    starts = (col ^ jnp.arange(4, dtype=jnp.int32)) * feat
    pieces = call(
        functools.partial(split_kernel, spans),
        [HBM],
        [shape((b - a, feat)) for a, b in spans],
        (tokens,),
        0,
        scratch=[pltpu.SemaphoreType.DMA((len(spans),))],
    )
    far_parts = []
    for piece in pieces:
        far_parts.append(over_col(piece, 2))
    near = over_col(tokens, 1)
    block_ids, block_counts, _ = lax.optimization_barrier(
        (block_ids, block_counts, pieces[0])
    )
    positions = (tok * tok_rows + jnp.arange(tok_rows, dtype=jnp.int32)).astype(f32)
    cosine, sine = turn_tables(positions)
    live = jnp.arange(nsel, dtype=jnp.int32)[None, None, :] < block_counts[:, :, None]
    owner, inside = block_ids // qblocks, block_ids % qblocks
    slot = (tok // 2 - owner // 2) * 2 + ((owner % 2) ^ (tok % 2))
    own = jnp.arange(qblocks, dtype=jnp.int32)[None, :, None] * BLK
    offsets = jnp.where(live, slot * tok_rows + inside * BLK, own).reshape(-1)
    counts = block_counts.reshape(-1)
    starts, cosine, sine, offsets, counts = lax.optimization_barrier(
        (starts, cosine, sine, offsets, counts)
    )
    out_own_near, out_send_near, out_own_far, out_send_far = call(
        columns_kernel,
        [SMEM, HBM],
        [shape((inner, feat))] * 4,
        (starts, w_out),
        0,
        scratch=[pltpu.SemaphoreType.DMA((4,))],
    )
    partner_near = over_col(out_send_near, 1)
    partner_far = over_col(out_send_far, 1)
    *weights, order = call(
        functools.partial(rows_kernel, (heads, qblocks, cuts, nsel // GROUP_BLOCKS)),
        [SMEM, SMEM, HBM, HBM, HBM],
        [shape((feat, width))] * 4 + [shape((heads * qblocks + 1,), jnp.int32)],
        (starts, counts, *ws),
        0,
        scratch=[pltpu.SemaphoreType.DMA((12,))],
    )
    sums = call(
        functools.partial(near_kernel, spans),
        [VMEM] * 4,
        [shape((b - a, width), f32) for a, b in spans],
        (tokens, near, weights[0], weights[1]),
        4 * tok_rows * feat * width,
    )

    queries = []
    shards = [[] for _ in range(toks)]
    for (a, b), far, summed in zip(spans, far_parts, sums):
        rows = b - a
        opposite = over_col(far, 1)
        summed = call(
            far_kernel,
            [VMEM] * 3,
            shape((rows, width), f32),
            (far, summed, weights[2]),
            2 * rows * feat * width,
        )
        query, pair = call(
            functools.partial(last_kernel, a, b),
            [VMEM] * 5,
            [shape((rows, heads * HEAD_SIZE)), shape((rows, 2 * HEAD_SIZE))],
            (opposite, summed, cosine, sine, weights[3]),
            2 * rows * feat * width,
        )
        queries.append(query)
        for line in range(lines):
            moved = pair
            if line:
                moved = up(pair, line)
            shards[2 * line + 1].append(across(moved))
            shards[2 * line].append(moved)
    parts = [piece for shard in shards for piece in shard]

    keeps, arrivals = [], []
    lists = (offsets, counts, order)
    out_spans = [(first * BLK, last * BLK) for first, last in cuts]
    for part, (first, last) in enumerate(cuts):
        rows = (last - first) * BLK
        attended = attend(
            lists, queries, parts, (first, last, qblocks), nsel, spans, part == 0
        )
        if part == 0:
            attended, gathered = attended
            parts = [gathered]
        partner = over_col(attended, 1)

        def project(own_w, partner_w, kind):
            return call(
                out_kernel,
                [VMEM] * 4,
                shape((rows, feat), kind),
                (attended, partner, own_w, partner_w),
                4 * rows * feat * inner,
            )

        sent = project(out_own_far, partner_far, bf16)
        arrivals.append(over_col(sent, 2))
        keeps.append(project(out_own_near, partner_near, f32))
    return call(
        functools.partial(final_kernel, out_spans),
        [VMEM] * (2 * len(out_spans)),
        shape((tok_rows, feat)),
        (*keeps, *arrivals),
        tok_rows * feat,
    )


def solution(mesh):
    in_specs = (
        P("tok", "col"),
        P(None, "col"),
        P(None, "col"),
        P(None, "col"),
        P("col", None),
        P("col", "tok", None),
        P("col", "tok"),
    )

    def body(*args):
        return on_device(mesh, *args)

    return jax.shard_map(
        body,
        mesh=mesh,
        in_specs=in_specs,
        out_specs=P("tok", "col"),
        check_vma=False,
    )
```

```python
import functools
import math

import jax
import jax.numpy as jnp
from jax import lax
from jax.experimental import pallas as pl
from jax.experimental.pallas import tpu as pltpu
from jax.sharding import PartitionSpec as P


HEAD_SIZE = 128
BLK = 64
GROUP_BLOCKS = 4
ROPE_BASE = 500000.0
NEG = -1e30
CODE = 256


SMEM = pl.BlockSpec(memory_space=pltpu.SMEM)
VMEM = pl.BlockSpec(memory_space=pltpu.VMEM)
HBM = pl.BlockSpec(memory_space=pltpu.HBM)

bf16, f32 = jnp.bfloat16, jnp.float32


def shape(dims, kind=bf16):
    return jax.ShapeDtypeStruct(dims, kind)


def call(kernel, ins, outs, args, flops, scratch=(), vmem=10, grown=0, out_spec=VMEM, aliases=()):
    args = [
        pltpu.with_memory_space_constraint(arg, pltpu.HBM) if spec is HBM else arg
        for spec, arg in zip(ins, args)
    ]
    moved = sum(x.size * x.dtype.itemsize for x in jax.tree.leaves((outs, args)))
    return pl.pallas_call(
        kernel,
        out_shape=outs,
        in_specs=ins,
        out_specs=jax.tree.map(lambda x: SMEM if x.dtype == jnp.int32 else out_spec, outs),
        input_output_aliases=dict(aliases),
        scratch_shapes=list(scratch),
        compiler_params=pltpu.CompilerParams(vmem_limit_bytes=vmem << 20),
        cost_estimate=pl.CostEstimate(
            flops=flops, transcendentals=grown, bytes_accessed=moved
        ),
    )(*args)


def dot(a, b):
    return jnp.dot(a, b, preferred_element_type=f32)


def turn_tables(positions):
    half = HEAD_SIZE // 2
    freq = ROPE_BASE ** (-jnp.arange(half, dtype=f32) / half)
    angle = positions[:, None] * freq[None, :]
    cosine, sine = jnp.cos(angle), jnp.sin(angle)
    return (
        jnp.concatenate([cosine, cosine], axis=1),
        jnp.concatenate([-sine, sine], axis=1),
    )


def run_copies(pairs, sem, meanwhile=lambda: None):
    copies = [
        pltpu.make_async_copy(source, target, sem.at[index])
        for index, (source, target) in enumerate(pairs)
    ]
    for copy in copies:
        copy.start()
    meanwhile()
    for copy in copies:
        copy.wait()


def split_kernel(spans, tokens, *rest):
    outs, sem = rest[:-1], rest[-1]
    run_copies(
        [(tokens.at[pl.ds(a, b - a)], out) for (a, b), out in zip(spans, outs)], sem
    )


def columns_kernel(starts_ref, wo, *rest):
    outs, sem = rest[:-1], rest[-1]
    feat = outs[0].shape[1]
    run_copies(
        [
            (wo.at[:, pl.ds(pl.multiple_of(starts_ref[index], feat), feat)], out)
            for index, out in enumerate(outs)
        ],
        sem,
    )


def sort_rows(counts_ref, order_ref, heads, qblocks, cuts, groups):
    for first, last in cuts:
        members = [(head, block) for head in range(heads) for block in range(first, last)]
        needed = [
            (counts_ref[head * qblocks + block] + GROUP_BLOCKS - 1) // GROUP_BLOCKS
            for head, block in members
        ]
        at = jnp.int32(first * heads)
        for wanted in range(groups, 0, -1):
            for (head, block), need in zip(members, needed):
                order_ref[at] = jnp.int32(head * CODE + block)
                at = at + (need == wanted).astype(jnp.int32)


def rows_kernel(sorting, starts_ref, counts_ref, *rest):
    sources, outs, order_ref, sem = rest[:3], rest[3:-2], rest[-2], rest[-1]
    feat = outs[0].shape[0]
    pairs = []
    for index, out in enumerate(outs):
        rows = pl.ds(pl.multiple_of(starts_ref[index], feat), feat)
        at = 0
        for source in sources:
            width = source.shape[1]
            pairs.append((source.at[rows, :], out.at[:, pl.ds(at, width)]))
            at += width
    run_copies(pairs, sem, lambda: sort_rows(counts_ref, order_ref, *sorting))


def near_kernel(spans, own_ref, near_ref, w0, w1, *outs):
    for (a, b), out in zip(spans, outs):
        out[...] = dot(own_ref[a:b], w0[...]) + dot(near_ref[a:b], w1[...])


def far_kernel(far_ref, sum_ref, w, out_ref):
    out_ref[...] = sum_ref[...] + dot(far_ref[...], w[...])


def last_kernel(a, b, far_ref, sum_ref, cos_ref, sin_ref, w, q_ref, kv_ref):
    product = sum_ref[...] + dot(far_ref[...], w[...])
    cosine, sine = cos_ref[a:b], sin_ref[a:b]
    width = q_ref.shape[1]
    for at in range(0, width + HEAD_SIZE, HEAD_SIZE):
        piece = product[:, at : at + HEAD_SIZE]
        turned = piece * cosine + pltpu.roll(piece, HEAD_SIZE // 2, 1) * sine
        if at < width:
            turned = turned * (HEAD_SIZE**-0.5 * math.log2(math.e))
            q_ref[:, at : at + HEAD_SIZE] = turned.astype(bf16)
        else:
            kv_ref[:, :HEAD_SIZE] = turned.astype(bf16)
    kv_ref[:, HEAD_SIZE:] = product[:, width + HEAD_SIZE :].astype(bf16)


def out_kernel(own_ref, partner_ref, own_w, partner_w, out_ref):
    total = dot(own_ref[...], own_w[...]) + dot(partner_ref[...], partner_w[...])
    out_ref[...] = total.astype(out_ref.dtype)


def final_kernel(a, kept, arrived, *rest):
    out_ref, held, sem = rest[-3:]
    half = held.shape[0] // 2
    copies = []
    for index in range(2):
        at = slice(index * half, (index + 1) * half)
        held[at] = (kept[at] + arrived[at].astype(f32)).astype(bf16)
        copy = pltpu.make_async_copy(
            held.at[at], out_ref.at[pl.ds(a + index * half, half)], sem.at[index]
        )
        copy.start()
        copies.append(copy)
    for copy in copies:
        copy.wait()


def attend_kernel(heads, place, nsel, spans, fresh, count, *refs):
    first, last, qblocks = place
    offsets_ref, counts_ref, order_ref = refs[:3]
    queries, parts = refs[3 : 3 + len(spans)], refs[3 + len(spans) : 3 + count]
    if fresh:
        out_ref, kv_ref, q_ref, o_ref = refs[3 + count :]
        at = 0
        for part in parts:
            kv_ref[at : at + part.shape[0]] = part[...]
            at += part.shape[0]
    else:
        out_ref, q_ref, o_ref = refs[3 + count :]
        (kv_ref,) = parts
    for head in range(heads):
        columns = slice(head * HEAD_SIZE, (head + 1) * HEAD_SIZE)
        for (a, b), part in zip(spans, queries):
            q_ref[head, a:b] = part[:, columns]
    width = GROUP_BLOCKS * BLK

    def some_rows(start, groups):
        lane = lax.broadcasted_iota(jnp.int32, (BLK, width), 1)
        row = lax.broadcasted_iota(jnp.int32, (BLK, width), 0)
        causal = (lane >= BLK) | (lane <= row)
        ones = jnp.ones((groups * width, HEAD_SIZE), bf16)
        places, scores, values = [], [], []
        for member in range(heads):
            code = order_ref[start + member]
            head, block = code // CODE, code % CODE
            index = head * qblocks + block
            query = q_ref[head, pl.ds(pl.multiple_of(block * BLK, BLK), BLK)]
            live = counts_ref[index]
            places.append((head, block))
            scores.append([])
            values.append([])
            for group in range(groups):
                pieces = []
                for slot in range(GROUP_BLOCKS):
                    at = offsets_ref[index * nsel + group * GROUP_BLOCKS + slot]
                    pieces.append(kv_ref[pl.ds(pl.multiple_of(at, BLK), BLK), :])
                both = jnp.concatenate(pieces, axis=0)
                values[-1].append(both[:, HEAD_SIZE:])
                score = lax.dot_general(
                    query,
                    both[:, :HEAD_SIZE],
                    (((1,), (1,)), ((), ())),
                    preferred_element_type=f32,
                )
                allowed = lane < (live - group * GROUP_BLOCKS) * BLK
                if group == 0:
                    allowed = allowed & causal
                scores[-1].append(jnp.where(allowed, score, NEG))
        highest = [
            jnp.max(functools.reduce(jnp.maximum, score), axis=-1, keepdims=True)
            for score in scores
        ]
        for (head, block), score, high, value in zip(places, scores, highest, values):
            weights = jnp.concatenate(
                [jnp.exp2(piece - high).astype(bf16) for piece in score], axis=1
            )
            both = dot(
                weights, jnp.concatenate([jnp.concatenate(value, axis=0), ones], axis=1)
            )
            target = pl.ds(pl.multiple_of((block - first) * BLK, BLK), BLK)
            o_ref[head, target] = (both[:, :HEAD_SIZE] / both[:, HEAD_SIZE:]).astype(bf16)

    def one_batch(batch, carry):
        start = first * heads + batch * heads
        code = order_ref[start]
        live = counts_ref[code // CODE * qblocks + code % CODE]
        needed = (live + GROUP_BLOCKS - 1) // GROUP_BLOCKS
        for groups in range(1, nsel // GROUP_BLOCKS + 1):

            @pl.when(needed == groups)
            def _(groups=groups):
                some_rows(start, groups)

        return carry

    lax.fori_loop(0, last - first, one_batch, 0)
    for head in range(heads):
        out_ref[:, head * HEAD_SIZE : (head + 1) * HEAD_SIZE] = o_ref[head]


def attend(lists, queries, parts, place, nsel, spans, fresh):
    heads = queries[0].shape[1] // HEAD_SIZE
    first, last, _ = place
    rows = (last - first) * BLK
    whole = spans[-1][1]
    keys = sum(part.shape[0] for part in parts)
    held = keys * HEAD_SIZE * 4 >> 20
    out = shape((rows, heads * HEAD_SIZE))
    pairs = rows * heads * nsel * BLK
    return call(
        functools.partial(
            attend_kernel, heads, place, nsel, spans, fresh, len(queries) + len(parts)
        ),
        [SMEM] * len(lists) + [VMEM] * (len(queries) + len(parts)),
        [out, shape((keys, 2 * HEAD_SIZE))] if fresh else out,
        (*lists, *queries, *parts),
        4 * pairs * HEAD_SIZE,
        scratch=[
            pltpu.VMEM((heads, whole, HEAD_SIZE), bf16),
            pltpu.VMEM((heads, rows, HEAD_SIZE), bf16),
        ],
        vmem=8 + 3 * held,
        grown=pairs,
    )


def on_device(mesh, tokens, w_query, w_key, w_value, w_out, block_ids, block_counts):
    cols, toks = mesh.shape["col"], mesh.shape["tok"]
    tok_rows, feat = tokens.shape
    heads = w_query.shape[1] // HEAD_SIZE
    qblocks, nsel = block_ids.shape[1:]
    col = lax.axis_index("col")
    tok = lax.axis_index("tok")
    lines = toks // 2
    inner = w_out.shape[0]
    ws = (w_query, w_key, w_value)
    width = sum(w.shape[1] for w in ws)

    def over_col(value, flip):
        return lax.ppermute(value, "col", [(i, i ^ flip) for i in range(cols)])

    def across(value):
        return lax.ppermute(value, "tok", [(i, i ^ 1) for i in range(toks)])

    def up(value, steps):
        return lax.ppermute(
            value, "tok", [(i, (i + 2 * steps) % toks) for i in range(toks)]
        )

    first = (qblocks + 1) // 2 * BLK
    spans = [(0, first), (first, tok_rows)]
    cuts = [(0, qblocks // 2), (qblocks // 2, qblocks)]
    starts = (col ^ jnp.arange(4, dtype=jnp.int32)) * feat
    pieces = []
    for span in spans:
        pieces += call(
            functools.partial(split_kernel, [span]),
            [HBM],
            [shape((span[1] - span[0], feat))],
            (tokens,),
            0,
            scratch=[pltpu.SemaphoreType.DMA((1,))],
        )
    far_parts = []
    for piece in pieces:
        far_parts.append(over_col(piece, 2))
    near = over_col(tokens, 1)
    block_ids, block_counts, _ = lax.optimization_barrier(
        (block_ids, block_counts, pieces[0])
    )
    positions = (tok * tok_rows + jnp.arange(tok_rows, dtype=jnp.int32)).astype(f32)
    cosine, sine = turn_tables(positions)
    live = jnp.arange(nsel, dtype=jnp.int32)[None, None, :] < block_counts[:, :, None]
    owner, inside = block_ids // qblocks, block_ids % qblocks
    slot = (tok // 2 - owner // 2) * 2 + ((owner % 2) ^ (tok % 2))
    own = jnp.arange(qblocks, dtype=jnp.int32)[None, :, None] * BLK
    offsets = jnp.where(live, slot * tok_rows + inside * BLK, own).reshape(-1)
    counts = block_counts.reshape(-1)
    starts, cosine, sine, offsets, counts = lax.optimization_barrier(
        (starts, cosine, sine, offsets, counts)
    )
    out_own_near, out_send_near, out_own_far, out_send_far = call(
        columns_kernel,
        [SMEM, HBM],
        [shape((inner, feat))] * 4,
        (starts, w_out),
        0,
        scratch=[pltpu.SemaphoreType.DMA((4,))],
    )
    partner_near = over_col(out_send_near, 1)
    partner_far = over_col(out_send_far, 1)
    *weights, order = call(
        functools.partial(rows_kernel, (heads, qblocks, cuts, nsel // GROUP_BLOCKS)),
        [SMEM, SMEM, HBM, HBM, HBM],
        [shape((feat, width))] * 4 + [shape((heads * qblocks + 1,), jnp.int32)],
        (starts, counts, *ws),
        0,
        scratch=[pltpu.SemaphoreType.DMA((12,))],
    )
    sums = call(
        functools.partial(near_kernel, spans),
        [VMEM] * 4,
        [shape((b - a, width), f32) for a, b in spans],
        (tokens, near, weights[0], weights[1]),
        4 * tok_rows * feat * width,
    )

    queries = []
    shards = [[] for _ in range(toks)]
    for (a, b), far, summed in zip(spans, far_parts, sums):
        rows = b - a
        opposite = over_col(far, 1)
        summed = call(
            far_kernel,
            [VMEM] * 3,
            shape((rows, width), f32),
            (far, summed, weights[2]),
            2 * rows * feat * width,
        )
        query, pair = call(
            functools.partial(last_kernel, a, b),
            [VMEM] * 5,
            [shape((rows, heads * HEAD_SIZE)), shape((rows, 2 * HEAD_SIZE))],
            (opposite, summed, cosine, sine, weights[3]),
            2 * rows * feat * width,
        )
        queries.append(query)
        for line in range(lines):
            moved = pair
            if line:
                moved = up(pair, line)
            shards[2 * line + 1].append(across(moved))
            shards[2 * line].append(moved)
    parts = [piece for shard in shards for piece in shard]

    keeps, arrivals = [], []
    lists = (offsets, counts, order)
    out_spans = [(first * BLK, last * BLK) for first, last in cuts]
    for part, (first, last) in enumerate(cuts):
        rows = (last - first) * BLK
        attended = attend(
            lists, queries, parts, (first, last, qblocks), nsel, spans, part == 0
        )
        if part == 0:
            attended, gathered = attended
            parts = [gathered]
        partner = over_col(attended, 1)

        def project(own_w, partner_w, kind):
            return call(
                out_kernel,
                [VMEM] * 4,
                shape((rows, feat), kind),
                (attended, partner, own_w, partner_w),
                4 * rows * feat * inner,
            )

        sent = project(out_own_far, partner_far, bf16)
        arrivals.append(over_col(sent, 2))
        keeps.append(project(out_own_near, partner_near, f32))
    out = ()
    for part, ((a, b), kept, arrived) in enumerate(zip(out_spans, keeps, arrivals)):
        out = call(
            functools.partial(final_kernel, a),
            [VMEM, VMEM, HBM][: 3 if part else 2],
            shape((tok_rows, feat)),
            (kept, arrived, *out),
            (b - a) * feat,
            scratch=[pltpu.VMEM((b - a, feat), bf16), pltpu.SemaphoreType.DMA((2,))],
            out_spec=HBM,
            aliases={2: 0} if part else {},
        )
        out = (out,)
    return out[0]


def solution(mesh):
    in_specs = (
        P("tok", "col"),
        P(None, "col"),
        P(None, "col"),
        P(None, "col"),
        P("col", None),
        P("col", "tok", None),
        P("col", "tok"),
    )

    def body(*args):
        return on_device(mesh, *args)

    return jax.shard_map(
        body,
        mesh=mesh,
        in_specs=in_specs,
        out_specs=P("tok", "col"),
        check_vma=False,
    )
```
